32 devices in a mesh: span: 8 (over z, x), slab: 4 (over y, core).
Axes of the slice: x: 2, y: 2, z: 4, core: 2. Of those that a mesh axis runs over, the one named last changes fastest.
Arguments:
- features: float32 [512, 32, 2048], P('slab', None, 'span'), may hold values from -6 to 6
- spectral_weight: float32 [512, 2048], P('span', 'slab'), may hold values from -2.5 to 2.5
- local_weight: float32 [32, 32], replicated, may hold values from -1 to 1
- bias_vector: float32 [32], replicated, may hold values from -1 to 1
Outputs:
- activated: float32 [512, 32, 2048], P('slab', None, 'span')
The draws below stay inside these ranges and needn't reach their ends.
All inputs are finite; a program needn't handle non-finite values.
Results may differ from the reference program's by a relative error of at most 0.00005.
Values sent between devices are 32-bit elements; how exact they have to be, the bound alone decides.
No kernel may reach another device: no remote copies, remote signals or barrier semaphores. Data moves between devices by JAX's collectives and lax.ppermute only.
A program may use at most 128 MiB of HBM per device.

```python
import jax
import jax.numpy as jnp
from jax import lax

C = 32
M = 512
NZ = 2048
ROWS = 512


def steps_of(key, dims, pieces, smallest, high):
    def one(dim, blocks):
        draws = jax.random.uniform(jax.random.fold_in(jax.random.fold_in(key, 6), dim), (blocks,), jnp.float32, smallest / len(pieces), high / len(pieces))
        return jnp.repeat(jnp.exp(draws), dims[dim] // blocks).reshape((-1,) + (1,) * (len(dims) - dim - 1))

    factor_of = one(*pieces[0])
    for cut in pieces[1:]:
        factor_of = factor_of * one(*cut)
    return factor_of


def bell_draw(rng, extent, scale, bound, split=(), kind=jnp.bfloat16):
    array = jax.random.normal(rng, extent, jnp.float32) * scale
    if len(split) > 0:
        array = steps_of(rng, extent, split, -0.22, 0.18) * array
    return jnp.clip(array, min=-bound, max=bound).astype(kind)


def setup_inputs(seed: int = 0) -> dict:
    key_of = jax.random.split(jax.random.key(seed), 5)
    features = bell_draw(key_of[0], (ROWS, C, NZ), 1.0, 6.0, ((0, 4), (2, 8)), jnp.float32)
    spectral_weight = bell_draw(key_of[1], (M, 2 * C * C), ((NZ / (4 * C * M)) ** 0.5), 2.5, ((0, 8), (1, 4)), jnp.float32)
    local_weight = bell_draw(key_of[2], (C, C), C ** -0.5, 1.0, (), jnp.float32)
    bias_vector = jnp.clip(jax.random.uniform(key_of[3], (C,), jnp.float32, -1.0, 1.0), -1.0, 1.0)
    return dict(features=features, spectral_weight=spectral_weight, local_weight=local_weight, bias_vector=bias_vector)


def reference(features, spectral_weight, local_weight, bias_vector):
    weights = spectral_weight.reshape(M, 2, C, C)
    weight_real = weights[:, 0]
    weight_imag = weights[:, 1]
    highest = lax.Precision.HIGHEST

    def one_row(line_data):
        spectrum = jnp.fft.rfft(line_data, axis=-1)[:, :M]
        spec_real = jnp.real(spectrum)
        spec_imag = jnp.imag(spectrum)
        mixed_real = jnp.einsum('cm,mco->om', spec_real, weight_real, precision=highest) - jnp.einsum('cm,mco->om', spec_imag, weight_imag, precision=highest)
        mixed_imag = jnp.einsum('cm,mco->om', spec_real, weight_imag, precision=highest) + jnp.einsum('cm,mco->om', spec_imag, weight_real, precision=highest)
        padded = jnp.pad(lax.complex(mixed_real, mixed_imag), ((0, 0), (0, NZ // 2 + 1 - M)))
        spectral = jnp.fft.irfft(padded, n=NZ, axis=-1)
        local_term = jnp.dot(local_weight.T, line_data, precision=highest, preferred_element_type=line_data.dtype)
        return jax.nn.gelu(spectral + local_term + bias_vector[:, None], approximate=False)

    return lax.map(one_row, features)
```

```python
import functools
import math

import jax
import jax.numpy as jnp
from jax import lax
from jax.experimental import pallas as pl
from jax.experimental.pallas import tpu as pltpu
from jax.sharding import PartitionSpec as P

HIGHEST = lax.Precision.HIGHEST
CHUNKS = 2
ROWS_AT_ONCE = 4


def turn(index, count):
    quarter = index % count * 4
    if quarter % count == 0:
        return ((1.0, 0.0), (0.0, 1.0), (-1.0, 0.0), (0.0, -1.0))[quarter // count]
    angle = 2.0 * math.pi * (index % count) / count
    return math.cos(angle), math.sin(angle)


def plus(total, factor, value):
    if factor == 0.0:
        return total
    if total is None:
        return value if factor == 1.0 else value * factor
    if factor == 1.0:
        return total + value
    if factor == -1.0:
        return total - value
    return total + value * factor


def split_residues(cells, count):
    half = count // 2
    even = [None] + [cells[s] + cells[count - s] for s in range(1, half)]
    odd = [None] + [cells[s] - cells[count - s] for s in range(1, half)]
    ends = (cells[0] + cells[half], cells[0] - cells[half])
    reals, imags = [], []
    for residue in range(half + 1):
        real, imag = ends[residue % 2], None
        for s in range(1, half):
            cos, sin = turn(residue * s, count)
            real = plus(real, cos, even[s])
            imag = plus(imag, -sin, odd[s])
        reals.append(real)
        imags.append(imag)
    return reals, imags


def join_residues(reals, imags, count):
    half = count // 2
    ends = (reals[0] + reals[half], reals[0] - reals[half])
    cells = [None] * count
    for s in range(half + 1):
        even, odd = ends[s % 2], None
        for residue in range(1, half):
            cos, sin = turn(residue * s, count)
            even = plus(even, cos, reals[residue])
            odd = plus(odd, sin, imags[residue])
        if s in (0, half):
            cells[s] = even
        else:
            cells[s] = even - odd
            cells[count - s] = even + odd
    return cells


def residue_pairs(count):
    half = count // 2
    return [(0, half)] + [(residue, count - residue) for residue in range(1, half)]


def residue_tables(count, modes_each, cells):
    total = count * cells
    first, second = (jnp.array(side, jnp.int32) for side in zip(*residue_pairs(count)))
    comb = lax.iota(jnp.int32, modes_each) * count
    modes = jnp.stack([first[:, None] + comb, second[:, None] + comb], axis=1)
    modes = modes.reshape(count // 2, 1, 2 * modes_each)
    phases = modes * lax.iota(jnp.int32, cells)[None, :, None] % total
    angles = phases.astype(jnp.float32) * (2.0 * math.pi / total)
    cos, sin = jnp.cos(angles), jnp.sin(angles)
    lane = lax.broadcasted_iota(jnp.int32, (1, 1, 2 * modes_each), 2)
    ends = lax.broadcasted_iota(jnp.int32, (count // 2, 1, 1), 0) == 0
    second_comb = lane >= modes_each
    from_real = jnp.where(ends & second_comb, 0.0, 1.0)
    upper = jnp.concatenate([cos * from_real, -sin * from_real], axis=2)
    sign = jnp.where(second_comb, -1.0, 1.0)
    lower = jnp.where(
        ends,
        jnp.concatenate([jnp.where(second_comb, cos, 0.0), jnp.where(second_comb, -sin, 0.0)], axis=2),
        jnp.concatenate([sin * sign, cos * sign], axis=2),
    )
    return jnp.concatenate([upper, lower], axis=1)


def spectral_kernel(count, me_ref, *refs):
    parts, (mix_hbm, table_hbm, scale_ref), outs = refs[:count], refs[count : count + 3], refs[count + 3 : 2 * count + 3]
    cells_ref, work, modes_real, modes_imag, mixed, mix_ref, table_ref, in_sems, out_sems, mix_sem, table_sem = refs[
        2 * count + 3 :
    ]
    _, lines, cells = cells_ref.shape
    pairs, width = count // 2, modes_real.shape[1]
    blocks, _, block_rows, _ = mix_ref.shape
    channels = math.isqrt(blocks * block_rows // 2)
    rows = lines // channels
    me = me_ref[0]
    step = 8

    fetches = [
        pltpu.make_async_copy(parts[d], cells_ref.at[me ^ d], in_sems.at[d]) for d in range(count)
    ]
    for fetch in fetches:
        fetch.start()
    table_fetch = pltpu.make_async_copy(table_hbm, table_ref, table_sem)
    table_fetch.start()
    mix_fetch = pltpu.make_async_copy(mix_hbm, mix_ref, mix_sem)
    mix_fetch.start()
    for fetch in fetches:
        fetch.wait()

    def forward(block, carry):
        at = pl.ds(pl.multiple_of(block * step, step), step)
        reals, imags = split_residues([cells_ref[s, at, :] for s in range(count)], count)
        for pair, (residue, other) in enumerate(residue_pairs(count)):
            work[pair, at, :cells] = reals[residue]
            work[pair, at, cells:] = reals[other] if pair == 0 else imags[residue]
        return carry

    lax.fori_loop(0, lines // step, forward, 0)
    table_fetch.wait()
    mix_fetch.wait()

    at_once = math.gcd(rows, ROWS_AT_ONCE)

    def one_pair(pair, carry):
        modes = jnp.dot(work[pair], table_ref[pair], precision=HIGHEST, preferred_element_type=jnp.float32)
        modes_real[...] = modes[:, :width]
        modes_imag[...] = modes[:, width:]
        scale = scale_ref[pair]

        def some_rows(group, inner):
            row = group * at_once

            def one_channel(channel, sums):
                weights = []
                for part in range(2):
                    column = part * channels * channels + channel * channels
                    at = pl.ds(pl.multiple_of(column % block_rows, channels), channels)
                    weights.append(mix_ref[column // block_rows, pair, at, :])
                real_weight, imag_weight = weights
                new = []
                for r in range(at_once):
                    line = pl.ds((row + r) * channels + channel, channels, stride=0)
                    real = modes_real[line, :]
                    imag = modes_imag[line, :]
                    new.append(sums[2 * r] + (real * real_weight - imag * imag_weight))
                    new.append(sums[2 * r + 1] + (real * imag_weight + imag * real_weight))
                return tuple(new)

            zero = jnp.zeros((channels, width), jnp.float32)
            sums = lax.fori_loop(0, channels, one_channel, (zero,) * (2 * at_once), unroll=4)
            for r in range(at_once):
                line = pl.ds(pl.multiple_of((row + r) * channels, channels), channels)
                mixed[line, :width] = sums[2 * r] * scale
                mixed[line, width:] = sums[2 * r + 1] * scale
            return inner

        lax.fori_loop(0, rows // at_once, some_rows, 0)
        work[pair] = lax.dot_general(
            mixed[...], table_ref[pair], (((1,), (1,)), ((), ())), precision=HIGHEST, preferred_element_type=jnp.float32
        )
        return carry

    lax.fori_loop(0, pairs, one_pair, 0)

    def backward(block, carry):
        at = pl.ds(pl.multiple_of(block * step, step), step)
        reals = [work[pair, at, :cells] for pair in range(pairs)]
        imags = [work[pair, at, cells:] for pair in range(pairs)]
        joined = join_residues(reals + [imags[0]], imags, count)
        for s in range(count):
            cells_ref[s, at, :] = joined[s]
        return carry

    lax.fori_loop(0, lines // step, backward, 0)
    stores = [pltpu.make_async_copy(cells_ref.at[me ^ d], outs[d], out_sems.at[d]) for d in range(count)]
    for store in stores:
        store.start()
    for store in stores:
        store.wait()


def spectral_term(me, parts, mixing, tables, scale):
    count = len(parts)
    lines, width = parts[0].shape
    columns = tables.shape[2]
    anywhere = pl.BlockSpec(memory_space=pl.ANY)
    return pl.pallas_call(
        functools.partial(spectral_kernel, count),
        out_shape=[jax.ShapeDtypeStruct((lines, width), jnp.float32)] * count,
        in_specs=[pl.BlockSpec(memory_space=pltpu.SMEM)]
        + [anywhere] * (count + 2)
        + [pl.BlockSpec(memory_space=pltpu.VMEM)],
        out_specs=[anywhere] * count,
        scratch_shapes=[
            pltpu.VMEM((count, lines, width), jnp.float32),
            pltpu.VMEM((count // 2, lines, 2 * width), jnp.float32),
            pltpu.VMEM((lines, columns // 2), jnp.float32),
            pltpu.VMEM((lines, columns // 2), jnp.float32),
            pltpu.VMEM((lines, columns), jnp.float32),
            pltpu.VMEM(mixing.shape, jnp.float32),
            pltpu.VMEM(tables.shape, jnp.float32),
            pltpu.SemaphoreType.DMA((count,)),
            pltpu.SemaphoreType.DMA((count,)),
            pltpu.SemaphoreType.DMA,
            pltpu.SemaphoreType.DMA,
        ],
        compiler_params=pltpu.CompilerParams(vmem_limit_bytes=48 << 20),
        cost_estimate=pl.CostEstimate(
            flops=24 * count * lines * width * columns // 2,
            bytes_accessed=4 * (2 * count * lines * width + mixing.size + tables.size),
            transcendentals=0,
        ),
        name="spectral",
    )(me, *parts, mixing, tables, scale)


def transpose_kernel(count, weights_ref, out_ref):
    combs = weights_ref.shape[0] // count
    for pair, both in enumerate(residue_pairs(count)):
        rows = [weights_ref[pl.ds(residue, combs, stride=count), :] for residue in both]
        out_ref[pair] = jnp.concatenate(rows, axis=0).T


def transpose_weights(weights, count):
    modes, columns = weights.shape
    at_once = math.gcd(columns, 128)
    return pl.pallas_call(
        functools.partial(transpose_kernel, count),
        out_shape=jax.ShapeDtypeStruct((count // 2, columns, 2 * modes // count), jnp.float32),
        grid=(columns // at_once,),
        in_specs=[pl.BlockSpec((modes, at_once), lambda i: (0, i))],
        out_specs=pl.BlockSpec((count // 2, at_once, 2 * modes // count), lambda i: (0, i, 0)),
        cost_estimate=pl.CostEstimate(flops=4 * weights.size, bytes_accessed=8 * weights.size, transcendentals=0),
        name="transpose",
    )(weights)


def local_kernel(weight_ref, bias_ref, cells_ref, out_ref):
    out_ref[...] = (
        jnp.dot(weight_ref[...], cells_ref[...], precision=HIGHEST, preferred_element_type=jnp.float32) + bias_ref[...]
    )


def local_term(features, local_weight, bias_vector):
    rows, channels, width = features.shape
    group = math.gcd(rows, 256 // channels)
    lines = group * channels
    weight = jnp.kron(jnp.eye(group, dtype=jnp.float32), local_weight.T)
    bias = jnp.broadcast_to(jnp.tile(bias_vector, group)[:, None], (lines, width))
    whole = pl.BlockSpec((lines, lines), lambda i: (0, 0))
    block = pl.BlockSpec((lines, width), lambda i: (i, 0))
    return pl.pallas_call(
        local_kernel,
        grid=(rows // group,),
        out_shape=jax.ShapeDtypeStruct((rows * channels, width), jnp.float32),
        in_specs=[whole, pl.BlockSpec((lines, width), lambda i: (0, 0)), block],
        out_specs=block,
        cost_estimate=pl.CostEstimate(
            flops=12 * rows * channels * lines * width, bytes_accessed=8 * features.size, transcendentals=0
        ),
        name="local",
    )(weight, bias, features.reshape(rows * channels, width))


def finish_kernel(chunk, distances, me_ref, *refs):
    group = len(distances)
    parts, before, out = refs[:group], refs[group], refs[group + 1]
    spectral, rows, part_sems, row_sems, out_sems = refs[group + 2 :]
    count = before.shape[0] // CHUNKS
    at = [chunk * count + (me_ref[0] ^ d) for d in distances]
    fetches = []
    for i in range(group):
        fetches.append(pltpu.make_async_copy(parts[i], spectral.at[i], part_sems.at[i]))
        fetches.append(pltpu.make_async_copy(before.at[at[i]], rows.at[i], row_sems.at[i]))
    for fetch in fetches:
        fetch.start()
    stores = []
    for i in range(group):
        fetches[2 * i].wait()
        fetches[2 * i + 1].wait()
        total = spectral[i] + rows[i]
        spectral[i] = 0.5 * total * (1.0 + lax.erf(total * math.sqrt(0.5)))
        stores.append(pltpu.make_async_copy(spectral.at[i], out.at[at[i]], out_sems.at[i]))
        stores[i].start()
    for store in stores:
        store.wait()


def finish(me, parts, before, chunk, distances):
    group = len(distances)
    lines, width = parts[0].shape
    anywhere = pl.BlockSpec(memory_space=pl.ANY)
    return pl.pallas_call(
        functools.partial(finish_kernel, chunk, distances),
        in_specs=[pl.BlockSpec(memory_space=pltpu.SMEM)] + [anywhere] * (group + 1),
        out_specs=anywhere,
        out_shape=jax.ShapeDtypeStruct(before.shape, jnp.float32),
        input_output_aliases={group + 1: 0},
        scratch_shapes=[
            pltpu.VMEM((group, lines, width), jnp.float32),
            pltpu.VMEM((group, lines, width), jnp.float32),
            pltpu.SemaphoreType.DMA((group,)),
            pltpu.SemaphoreType.DMA((group,)),
            pltpu.SemaphoreType.DMA((group,)),
        ],
        compiler_params=pltpu.CompilerParams(vmem_limit_bytes=16 << 20),
        cost_estimate=pl.CostEstimate(
            flops=60 * group * lines * width, bytes_accessed=12 * group * lines * width, transcendentals=0
        ),
        name="finish",
    )(me, *parts, before)


def swap(value, axis, distance):
    count = lax.axis_size(axis)
    return lax.ppermute(value, axis, [(i, i ^ distance) for i in range(count)])


def join_halves(value, axis, distance, place):
    other = swap(value, axis, distance)
    lower = lax.axis_index(axis) & distance == 0
    return jnp.stack([jnp.where(lower, value, other), jnp.where(lower, other, value)], axis=place)


def gather_blocks(value, axis):
    shape = value.shape
    distance, place = lax.axis_size(axis) // 2, 0
    while distance > 0:
        value = join_halves(value, axis, distance, place)
        distance, place = distance // 2, place + 1
    return value.reshape(-1, *shape)


def gather_weights(weights, channels):
    columns = weights.shape[1]
    mine = gather_blocks(weights, "span").reshape(-1, columns)
    return gather_blocks(transpose_weights(mine, lax.axis_size("span")), "slab")


def crossing_first(count):
    far = range(count // 2, count)
    near = range(1, count // 2)
    return sorted(far, key=lambda d: d % 2) + sorted(near, key=lambda d: d % 2)


def shards(features, spectral_weight, local_weight, bias_vector):
    rows, channels, width = features.shape
    count = lax.axis_size("span")
    modes_dev = spectral_weight.shape[0]
    position = lax.axis_index("span")
    me = position.astype(jnp.int32).reshape(1)
    lines = rows // (CHUNKS * count) * channels
    blocks = features.reshape(CHUNKS, count, lines, width)
    mixing = gather_weights(spectral_weight, channels)
    order = crossing_first(count)

    def send(parts):
        got = {0: parts(0)}
        for d in order:
            got[d] = swap(parts(d), "span", d)
        return got

    arrived = []
    for chunk in range(CHUNKS):
        arrived.append(send(lambda d: lax.dynamic_index_in_dim(blocks[chunk], position ^ d, 0, keepdims=False)))
    tables = residue_tables(count, modes_dev, width)
    total = count * width
    lane = lax.broadcasted_iota(jnp.int32, (count // 2, 1, 2 * modes_dev), 2)
    pair = lax.broadcasted_iota(jnp.int32, (count // 2, 1, 2 * modes_dev), 0)
    scale = jnp.where((lane == 0) & (pair == 0), 1.0, 2.0).astype(jnp.float32) / total
    before = local_term(features, local_weight, bias_vector).reshape(CHUNKS * count, lines, width)
    returned = []
    for chunk in range(CHUNKS):
        term = spectral_term(me, [arrived[chunk][d] for d in range(count)], mixing, tables, scale)
        returned.append(send(lambda d: term[d]))
    for chunk in range(CHUNKS):
        near = list(range(count // 2))
        before = finish(me, [returned[chunk][d] for d in near], before, chunk, near)
        for d in order[: count // 2]:
            before = finish(me, [returned[chunk][d]], before, chunk, [d])
    return before.reshape(rows, channels, width)


def solution(mesh):
    placed = (P("slab", None, "span"), P("span", "slab"), P(), P())
    return jax.shard_map(
        shards, mesh=mesh, in_specs=placed, out_specs=P("slab", None, "span"), check_vma=False
    )
```
